256 devices in a mesh: grp: 8 (over z), dev: 32 (over x, y, core).
Axes of the slice: x: 4, y: 4, z: 8, core: 2. Of those that a mesh axis runs over, the one named last changes fastest.
Arguments:
- incident: bfloat16 [1024, 128, 128], P(('grp', 'dev')), may hold values from -6 to 6
- tmatrix: bfloat16 [1024, 128, 128], P(('grp', 'dev')), may hold values from -0.5 to 0.5
- blocks: bfloat16 [32768, 128, 128], P(('grp', 'dev')), may hold values from -0.09375 to 0.09375
- need: int32 [256, 32, 4], P(('grp', 'dev')), may hold values from 0 to 3, as said below
- pair_src: int32 [256, 512], P(('grp', 'dev')), may hold values from 0 to 127
- pair_tgt: int32 [256, 512], P(('grp', 'dev')), may hold values from 0 to 3
- pair_blk: int32 [256, 512], P(('grp', 'dev')), may hold values from 0 to 127
- pair_count: int32 [256], P(('grp', 'dev')), may hold values from 128 to 512, as said below
- factor: float32 [1024, 2048], P(('grp', 'dev')), may hold values from -24 to 24
- harmonics: bfloat16 [2048, 128], replicated, may hold values from -0.015625 to 0.015625
- owner: int32 [2048], replicated, may hold values from 0 to 2047, each once
Outputs:
- amplitudes: float32 [2048, 128], P(('grp', 'dev'))
The draws below stay inside these ranges and needn't reach their ends.
Inputs may be any that keep to these rules, and one draw needn't show every extreme that they name: Each row need[k, j] lists 4 distinct local spheres of peer j. `pair_count`: some device has exactly 512 live pairs.
All inputs are finite; a program needn't handle non-finite values.
Results may differ from the reference program's by a relative error of at most 0.0075.
Values may be sent and summed in bfloat16 or wider, within the bound.
No kernel may reach another device: no remote copies, remote signals or barrier semaphores. Data moves between devices by JAX's collectives and lax.ppermute only.
A program may use at most 128 MiB of HBM per device.

```python
import jax
import jax.numpy as jnp
from jax import lax

L = 128
Q = 128
NDIR = 2048
SPH_DEV = 4
CAP = 4
NBLK = 128
SWEEPS = 2
PAIR_MAX = 512
DEVS = 256
SPHERES = 1024
N_GRP = 8
N_DEV = 32


def draw_need(key, part):
    row_keys = jax.random.split(jax.random.fold_in(key, 11), DEVS * N_DEV)
    shuffled = jax.vmap(lambda row_key: jax.random.permutation(row_key, jnp.arange(SPH_DEV, dtype=jnp.int32)))(row_keys)
    return shuffled[:, :CAP].reshape(DEVS, N_DEV, CAP).astype(jnp.int32)


def draw_pair_count(key, part):
    key_base = jax.random.fold_in(key, 21)
    key_heavy = jax.random.fold_in(key, 22)
    key_busiest = jax.random.fold_in(key, 23)
    drawn = jax.random.randint(key_base, (DEVS,), PAIR_MAX // 4, PAIR_MAX // 2 + 1)
    is_heavy = jax.random.randint(key_heavy, (DEVS,), 0, 16) == 0
    counts = jnp.where(is_heavy, PAIR_MAX, drawn)
    busiest = jax.random.randint(key_busiest, (), 0, DEVS)
    counts = jnp.where(jnp.arange(DEVS) == busiest, PAIR_MAX, counts)
    return counts.astype(jnp.int32)


def set_ends(values, own_key, low, largest):
    extent = values.shape
    place = [jax.random.randint(jax.random.fold_in(own_key, axis), (), 0, extent[axis]) for axis in range(len(extent))]
    values = values.at[tuple(place)].set(low)
    longest = extent.index(max(extent))
    place[longest] = (place[longest] + 1) % extent[longest]
    return values.at[tuple(place)].set(largest)


def strengthened(drawn, own_key, source, target, parts, factor):
    def block_of(dim):
        return (jnp.arange(drawn.shape[dim]) // (drawn.shape[dim] // parts)).reshape((-1,) + (1,) * (drawn.ndim - 1 - dim))

    one_side = jax.random.permutation(own_key, parts)[block_of(target)]
    second = (block_of(target) + parts // 2) % parts
    return jnp.where((block_of(source) == one_side) | (block_of(source) == second), factor * drawn, drawn)


def level_of(stream_key, dims, cuts, low, top_value):
    loudness, own = 1.0, jax.random.fold_in(stream_key, 6)
    for dim, parts in cuts:
        heights = jnp.exp(jax.random.uniform(jax.random.fold_in(own, dim), (parts,), jnp.float32, low / len(cuts), top_value / len(cuts)))
        loudness = loudness * jnp.repeat(heights, dims[dim] // parts).reshape([-1 if axis == dim else 1 for axis in range(len(dims))])
    return loudness


def bell_draw(key, extent, scale, bound, cuts=(), kind=jnp.bfloat16):
    array = scale * jax.random.normal(key, extent, jnp.float32)
    if cuts:
        array = array * level_of(key, extent, cuts, -0.22, 0.18)
    return jnp.clip(array, -bound, bound).astype(kind)


def noise_with(rng, extent, width, most, cuts, heavy, kind=jnp.bfloat16):
    entries = width * jax.random.normal(rng, extent, jnp.float32)
    if cuts:
        entries = entries * level_of(rng, extent, cuts, -0.22, 0.18)
    return jnp.clip(strengthened(entries, jax.random.fold_in(rng, 3), *heavy), -most, most).astype(kind)


def setup_inputs(seed: int = 0) -> dict:
    key_list = jax.random.split(jax.random.key(seed), 12)
    return {
        "incident": bell_draw(key_list[0], (SPHERES, L, Q), 1.0, 6.0, ((0, 256),)),
        "tmatrix": bell_draw(key_list[1], (SPHERES, L, L), L ** -0.5, 0.5, ((0, 256),)),
        "blocks": bell_draw(key_list[2], (DEVS * NBLK, L, L), (L * 32) ** -0.5, 0.09375, ((0, 256),)),
        "need": draw_need(jax.random.fold_in(key_list[11], 71), 0),
        "pair_src": set_ends(jax.random.randint(key_list[4], (DEVS, PAIR_MAX), 0, N_DEV * CAP), jax.random.fold_in(key_list[4], 1), 0, (N_DEV * CAP) - 1).astype(jnp.int32),
        "pair_tgt": set_ends(jax.random.randint(key_list[5], (DEVS, PAIR_MAX), 0, SPH_DEV), jax.random.fold_in(key_list[5], 1), 0, SPH_DEV - 1).astype(jnp.int32),
        "pair_blk": set_ends(jax.random.randint(key_list[6], (DEVS, PAIR_MAX), 0, NBLK), jax.random.fold_in(key_list[6], 1), 0, NBLK - 1).astype(jnp.int32),
        "pair_count": draw_pair_count(jax.random.fold_in(key_list[11], 71), 0),
        "factor": noise_with(key_list[8], (SPHERES, NDIR), 1.0, 24.0, ((0, 256),), (0, 1, 256, 6.0), jnp.float32),
        "harmonics": bell_draw(key_list[9], (NDIR, L), (L * SPHERES) ** -0.5, 0.015625),
        "owner": jax.random.permutation(key_list[10], NDIR).astype(jnp.int32),
    }


def apply_tmatrix(tmatrix, field):
    product = jnp.einsum("skl,slq->skq", tmatrix.astype(jnp.float32), field.astype(jnp.float32), precision=lax.Precision.HIGHEST)
    return lax.optimization_barrier(product.astype(jnp.bfloat16))


def reference(incident, tmatrix, blocks, need, pair_src, pair_tgt, pair_blk, pair_count, factor, harmonics, owner):
    devices_all = N_GRP * N_DEV
    coeff = apply_tmatrix(tmatrix, incident)
    first_dev = (jnp.arange(devices_all, dtype=jnp.int32) // N_DEV) * N_DEV
    peer_ids = first_dev[:, None, None] + jnp.arange(N_DEV, dtype=jnp.int32)[None, :, None]
    global_ids = (peer_ids * SPH_DEV + need).reshape(devices_all, N_DEV * CAP).astype(jnp.int32)
    pair_global = jnp.take_along_axis(global_ids, pair_src, axis=1).astype(jnp.int32)
    blocks_dev = blocks.reshape(devices_all, NBLK, L, L)
    incident_wide = incident.astype(jnp.float32)
    for sweep_index in range(SWEEPS):
        def one_device(packed):
            source_ids, targets, block_ids, count, local_blocks = packed
            source_tiles = jnp.take(coeff, source_ids, axis=0).astype(jnp.float32)
            operators = jnp.take(local_blocks, block_ids, axis=0).astype(jnp.float32)
            contrib = jnp.einsum("pkl,plq->pkq", operators, source_tiles, precision=lax.Precision.HIGHEST)
            pair_live = jnp.arange(PAIR_MAX, dtype=jnp.int32) < count
            selector = ((targets[None, :] == jnp.arange(SPH_DEV, dtype=jnp.int32)[:, None]) & pair_live[None, :]).astype(jnp.float32)
            return jnp.einsum("sp,pkq->skq", selector, contrib, precision=lax.Precision.HIGHEST)

        scattered = lax.map(one_device, (pair_global, pair_tgt, pair_blk, pair_count, blocks_dev))
        scattered = scattered.reshape(SPHERES, L, Q)
        field = (incident_wide + scattered).astype(jnp.bfloat16)
        coeff = apply_tmatrix(tmatrix, field)
    coeff_dev = coeff.reshape(devices_all, SPH_DEV, L, Q)
    factor_dev = factor.reshape(devices_all, SPH_DEV, NDIR)
    table = harmonics.astype(jnp.float32)

    def accumulate(running, packed):
        local_factor, local_coeff = packed
        weighted = lax.optimization_barrier((local_factor[:, :, None] * table[None]).astype(jnp.bfloat16))
        term = jnp.einsum("sdl,slq->dq", weighted.astype(jnp.float32), local_coeff.astype(jnp.float32), precision=lax.Precision.HIGHEST)
        return running + term, None

    far, unused = lax.scan(accumulate, jnp.zeros((NDIR, Q), jnp.float32), (factor_dev, coeff_dev))
    return jnp.take(far, owner, axis=0)
```

```python
import jax
import jax.numpy as jnp
from jax import lax
from jax.experimental import pallas as pl
from jax.experimental.pallas import tpu as pltpu
from jax.sharding import PartitionSpec as P

SIDE = 4
OWN = 4
SOURCES = 2 * SIDE * SIDE * OWN
BLOCKS = 128
PAIRS = 512
TILE = 128
JOIN = 8
WIDE = 4
ROOM = PAIRS + JOIN
LISTS = 2 * OWN
GROUPS = PAIRS // JOIN + OWN + WIDE

SMEM = pl.BlockSpec(memory_space=pltpu.SMEM)
VMEM = pl.BlockSpec(memory_space=pltpu.VMEM)
ANY = pl.BlockSpec(memory_space=pl.ANY)


def device_of(x, y, core):
    return ((x % SIDE) * SIDE + y % SIDE) * 2 + core


def moves(step):
    spots = [(x, y, c) for x in range(SIDE) for y in range(SIDE) for c in range(2)]
    return [(device_of(*spot), device_of(*step(*spot))) for spot in spots]


def along_first(shift):
    return moves(lambda x, y, c: (x + shift, y, c) if c == 0 else (x, y + shift, c))


def along_second(shift):
    return moves(lambda x, y, c: (x, y + shift, c) if c == 0 else (x + shift, y, c))


SWAP = moves(lambda x, y, c: (x, y, 1 - c))


def send(values, pairs):
    return lax.ppermute(values, "dev", pairs)


def spread(coeff):
    half = OWN // 2
    first3 = send(coeff, along_first(1))
    first1 = send(coeff, along_first(-1))
    first2a = send(first3[:half], along_first(1))
    first2b = send(first1[half:], along_first(-1))
    row = jnp.concatenate([coeff, first1, first2a, first2b, first3])
    half = SIDE * OWN // 2
    second3 = send(row, along_second(1))
    second1 = send(row, along_second(-1))
    other0 = send(row, SWAP)
    second2a = send(second3[:half], along_second(1))
    second2b = send(second1[half:], along_second(-1))
    other3 = send(second3, SWAP)
    other1 = send(second1, SWAP)
    other2a = send(second2a, SWAP)
    other2b = send(second2b, SWAP)
    early = (row, second1, second3, other0, other1, other3)
    late = (second2a, second2b, other2a, other2b)
    return early, late


EARLY_AT = (0, 16, 48, 64, 80, 112)
LATE_AT = (32, 40, 96, 104)


def source_table(need):
    me = lax.axis_index("dev")
    peer = jnp.arange(2 * SIDE * SIDE, dtype=jnp.int32)
    core = peer & 1
    dx = ((peer >> 3) - (me >> 3)) & 3
    dy = (((peer >> 1) & 3) - ((me >> 1) & 3)) & 3
    first = jnp.where(core == 0, dx, dy)
    second = jnp.where(core == 0, dy, dx)
    slot = ((core ^ (me & 1)) << 6) + (second << 4) + (first << 2)
    late = jnp.where(second == 2, 1 << 20, 0)
    return ((slot + late)[:, None] + need).reshape(-1)


def plan_kernel(table, src, operand, count, lists, groups, sizes, filled):
    for k in range(LISTS):
        filled[k] = k * ROOM

    def place(p, carry):
        word = table[src[p]]
        tail = operand[p]
        which = (tail & 3) | (word >> 18)
        at = filled[which]
        lists[at] = word + (tail & 0x7F00)
        filled[which] = at + 1
        return carry

    lax.fori_loop(0, count[0], place, 0)
    for u in range(JOIN):
        lists[LISTS * ROOM + u] = SOURCES
    for part in range(2):
        total = jnp.int32(0)
        for k in range(part * OWN, (part + 1) * OWN):
            end = filled[k]
            for u in range(JOIN):
                lists[end + u] = SOURCES
            several = (end - k * ROOM + (JOIN - 1)) // JOIN

            def enter(g, carry, k=k, part=part, total=total):
                groups[part * GROUPS + total + g] = (k * ROOM + g * JOIN) | ((k % OWN) << 16)
                return carry

            lax.fori_loop(0, several, enter, 0)
            total = total + several
        for w in range(WIDE):
            groups[part * GROUPS + total + w] = LISTS * ROOM
        sizes[part] = (total + (WIDE - 1)) // WIDE


def plan(table, src, operand, count):
    return pl.pallas_call(
        plan_kernel,
        out_shape=(
            jax.ShapeDtypeStruct(((LISTS + 1) * ROOM,), jnp.int32),
            jax.ShapeDtypeStruct((2 * GROUPS,), jnp.int32),
            jax.ShapeDtypeStruct((2,), jnp.int32),
        ),
        in_specs=[SMEM] * 4,
        out_specs=(SMEM,) * 3,
        scratch_shapes=[pltpu.SMEM((LISTS,), jnp.int32)],
        cost_estimate=pl.CostEstimate(flops=5_000_000_000, bytes_accessed=16384, transcendentals=0),
        name="plan",
    )(table, src, operand, count)


def add_pairs(part, lists, groups, sizes, blocks, sources, total):
    def step(i, carry):
        made = []
        for w in range(WIDE):
            group = groups[part * GROUPS + i * WIDE + w]
            base = group & 0xFFFF
            left, right = [], []
            for u in range(JOIN):
                word = lists[base + u]
                left.append(blocks[(word >> 8) & 0x7F])
                right.append(sources[word & 0xFF])
            product = jnp.dot(
                jnp.concatenate(left, axis=1),
                jnp.concatenate(right, axis=0),
                preferred_element_type=jnp.float32,
            )
            made.append((group >> 16, product))
        for target, product in made:
            total[target] += product
        return carry

    lax.fori_loop(0, sizes[part], step, 0)


def fetch(pieces, places, sources, sems):
    copies = []
    for n, (piece, place) in enumerate(zip(pieces, places)):
        copy = pltpu.make_async_copy(piece, sources.at[pl.ds(place, piece.shape[0])], sems.at[n])
        copy.start()
        copies.append(copy)
    sources[SOURCES] = jnp.zeros((TILE, TILE), jnp.bfloat16)
    for copy in copies:
        copy.wait()


def early_kernel(lists, groups, sizes, blocks, incident, *rest):
    pieces, (total, sources, sems) = rest[:-3], rest[-3:]
    fetch(pieces, EARLY_AT, sources, sems)
    total[...] = incident[...].astype(jnp.float32)
    add_pairs(0, lists, groups, sizes, blocks, sources, total)


def finish(tmatrix, total, t):
    field = total[t].astype(jnp.bfloat16)
    return jnp.dot(tmatrix[t], field, preferred_element_type=jnp.float32).astype(jnp.bfloat16)


def late_kernel(lists, groups, sizes, blocks, before, tmatrix, *rest):
    pieces, (coeff, sources, total, sems) = rest[:-4], rest[-4:]
    fetch(pieces, LATE_AT, sources, sems)
    total[...] = before[...]
    add_pairs(1, lists, groups, sizes, blocks, sources, total)
    for t in range(OWN):
        coeff[t] = finish(tmatrix, total, t)


FAR_ROWS = 256


def last_kernel(lists, groups, sizes, blocks, before, tmatrix, weighted, *rest):
    pieces, (far, sources, total, coeff, sems) = rest[:-5], rest[-5:]
    fetch(pieces, LATE_AT, sources, sems)
    total[...] = before[...]
    add_pairs(1, lists, groups, sizes, blocks, sources, total)
    for t in range(OWN):
        coeff[pl.ds(t * TILE, TILE), :] = finish(tmatrix, total, t)

    def chunk(i, carry):
        rows = pl.ds(pl.multiple_of(i * FAR_ROWS, FAR_ROWS), FAR_ROWS)
        far[rows, :] = jnp.dot(weighted[rows, :], coeff[...], preferred_element_type=jnp.float32)
        return carry

    lax.fori_loop(0, far.shape[0] // FAR_ROWS, chunk, 0)


SCRATCH = pltpu.VMEM((SOURCES + 1, TILE, TILE), jnp.bfloat16)
TOTAL = (OWN, TILE, TILE)


def early_pairs(made, blocks, incident, pieces):
    return pl.pallas_call(
        early_kernel,
        out_shape=jax.ShapeDtypeStruct(TOTAL, jnp.float32),
        in_specs=[SMEM] * 3 + [VMEM] * 2 + [ANY] * len(pieces),
        out_specs=VMEM,
        scratch_shapes=[SCRATCH, pltpu.SemaphoreType.DMA((len(pieces),))],
        cost_estimate=pl.CostEstimate(
            flops=2_000_000_000, bytes_accessed=8_000_000, transcendentals=0
        ),
        name="early",
    )(*made, blocks, incident, *pieces)


def late_pairs(made, blocks, before, tmatrix, pieces):
    return pl.pallas_call(
        late_kernel,
        out_shape=jax.ShapeDtypeStruct(TOTAL, jnp.bfloat16),
        in_specs=[SMEM] * 3 + [VMEM] * 3 + [ANY] * len(pieces),
        out_specs=VMEM,
        scratch_shapes=[
            SCRATCH,
            pltpu.VMEM(TOTAL, jnp.float32),
            pltpu.SemaphoreType.DMA((len(pieces),)),
        ],
        name="late",
    )(*made, blocks, before, tmatrix, *pieces)


def last_pairs(made, blocks, before, tmatrix, weighted, pieces):
    return pl.pallas_call(
        last_kernel,
        out_shape=jax.ShapeDtypeStruct((weighted.shape[0], TILE), jnp.float32),
        in_specs=[SMEM] * 3 + [VMEM] * 4 + [ANY] * len(pieces),
        out_specs=VMEM,
        scratch_shapes=[
            SCRATCH,
            pltpu.VMEM(TOTAL, jnp.float32),
            pltpu.VMEM((OWN * TILE, TILE), jnp.bfloat16),
            pltpu.SemaphoreType.DMA((len(pieces),)),
        ],
        name="last",
    )(*made, blocks, before, tmatrix, weighted, *pieces)


def apply_tmatrix(tmatrix, field):
    product = jnp.einsum("skl,slq->skq", tmatrix, field, preferred_element_type=jnp.float32)
    return product.astype(jnp.bfloat16)


def body(
    incident,
    tmatrix,
    blocks,
    need,
    pair_src,
    pair_tgt,
    pair_blk,
    pair_count,
    factor,
    harmonics,
    owner,
):
    n_grp, n_dev = lax.axis_size("grp"), lax.axis_size("dev")
    coeff = apply_tmatrix(tmatrix, incident)
    made = plan(source_table(need[0]), pair_src[0], pair_tgt[0] | (pair_blk[0] << 8), pair_count)
    early, late = spread(coeff)
    before = early_pairs(made, blocks, incident, early)
    coeff = late_pairs(made, blocks, before, tmatrix, late)

    rows = owner.shape[0] // (n_grp * n_dev)
    order = owner.reshape(n_grp, n_dev, rows).transpose(1, 0, 2).reshape(-1)
    table = jnp.take(harmonics, order, axis=0).astype(jnp.float32)
    phases = jnp.take(factor, order, axis=1)
    weighted = (phases.T[:, :, None] * table[:, None, :]).astype(jnp.bfloat16)
    weighted = weighted.reshape(owner.shape[0], -1)

    early, late = spread(coeff)
    before = early_pairs(made, blocks, incident, early)
    far = last_pairs(made, blocks, before, tmatrix, weighted, late)

    far = far.reshape(n_dev, n_grp * rows, TILE)
    far = lax.all_to_all(far, "dev", 0, 0).sum(axis=0)
    far = far.reshape(n_grp, rows, TILE)
    return lax.all_to_all(far, "grp", 0, 0).sum(axis=0)


def solution(mesh):
    both = ("grp", "dev")
    return jax.shard_map(
        body,
        mesh=mesh,
        in_specs=(
            P(both, None, None),
            P(both, None, None),
            P(both, None, None),
            P(both, None, None),
            P(both, None),
            P(both, None),
            P(both, None),
            P(both),
            P(both, None),
            P(),
            P(),
        ),
        out_specs=P(both, None),
        check_vma=False,
    )
```

```python
import jax
import jax.numpy as jnp
from jax import lax
from jax.experimental import pallas as pl
from jax.experimental.pallas import tpu as pltpu
from jax.sharding import PartitionSpec as P

SIDE = 4
OWN = 4
SOURCES = 2 * SIDE * SIDE * OWN
BLOCKS = 128
PAIRS = 512
TILE = 128
JOIN = 8
WIDE = 4
ROOM = PAIRS + JOIN
LISTS = 2 * OWN
GROUPS = PAIRS // JOIN + OWN + WIDE

LIMIT = pltpu.CompilerParams(vmem_limit_bytes=16 << 20)
SMEM = pl.BlockSpec(memory_space=pltpu.SMEM)
VMEM = pl.BlockSpec(memory_space=pltpu.VMEM)
ANY = pl.BlockSpec(memory_space=pl.ANY)


def device_of(x, y, core):
    return ((x % SIDE) * SIDE + y % SIDE) * 2 + core


def moves(step):
    spots = [(x, y, c) for x in range(SIDE) for y in range(SIDE) for c in range(2)]
    return [(device_of(*spot), device_of(*step(*spot))) for spot in spots]


def along_first(shift):
    return moves(lambda x, y, c: (x + shift, y, c) if c == 0 else (x, y + shift, c))


def along_second(shift):
    return moves(lambda x, y, c: (x, y + shift, c) if c == 0 else (x + shift, y, c))


SWAP = moves(lambda x, y, c: (x, y, 1 - c))


def send(values, pairs):
    return lax.ppermute(values, "dev", pairs)


def together(values, *fillers):
    return lax.optimization_barrier((values, fillers))[0]


def spread(coeff, fill_first, fill_second):
    half = OWN // 2
    first3 = send(coeff, along_first(1))
    first1 = send(coeff, along_first(-1))
    first3, first1 = together((first3, first1), fill_first)
    first2a = send(first3[:half], along_first(1))
    first2b = send(first1[half:], along_first(-1))
    first2a, first2b = together((first2a, first2b), fill_second)
    low = jnp.concatenate([coeff, first1])
    high = jnp.concatenate([first2a, first2b, first3])
    low3 = send(low, along_second(1))
    high1 = send(high, along_second(-1))
    high3 = send(high, along_second(1))
    low1 = send(low, along_second(-1))
    low2 = send(low3, along_second(1))
    high2 = send(high1, along_second(-1))
    near = (low, high, low1, high1, low3, high3)
    far = (low2, high2)
    return near, tuple(send(piece, SWAP) for piece in near), far


def swapped(pieces, before):
    pieces = together(pieces, before)
    return pieces + tuple(send(piece, SWAP) for piece in pieces)


NEAR_AT = (0, 8, 16, 24, 48, 56)
FAR_AT = (32, 40)
EARLY_AT = NEAR_AT + tuple(place + SOURCES // 2 for place in NEAR_AT)
LATE_AT = FAR_AT + tuple(place + SOURCES // 2 for place in FAR_AT)


def source_table(need):
    me = lax.axis_index("dev")
    peer = jnp.arange(2 * SIDE * SIDE, dtype=jnp.int32)
    core = peer & 1
    dx = ((peer >> 3) - (me >> 3)) & 3
    dy = (((peer >> 1) & 3) - ((me >> 1) & 3)) & 3
    first = jnp.where(core == 0, dx, dy)
    second = jnp.where(core == 0, dy, dx)
    slot = ((core ^ (me & 1)) << 6) + (second << 4) + (first << 2)
    late = jnp.where(second == 2, 1 << 20, 0)
    return ((slot + late)[:, None] + need).reshape(-1)


def plan_kernel(table, src, operand, count, lists, groups, sizes, filled):
    for k in range(LISTS):
        filled[k] = k * ROOM

    def place(p, carry):
        word = table[src[p]]
        tail = operand[p]
        which = (tail & 3) | (word >> 18)
        at = filled[which]
        lists[at] = word + (tail & 0x7F00)
        filled[which] = at + 1
        return carry

    lax.fori_loop(0, count[0], place, 0)
    for u in range(JOIN):
        lists[LISTS * ROOM + u] = SOURCES
    for part in range(2):
        total = jnp.int32(0)
        for k in range(part * OWN, (part + 1) * OWN):
            end = filled[k]
            for u in range(JOIN):
                lists[end + u] = SOURCES
            several = (end - k * ROOM + (JOIN - 1)) // JOIN

            def enter(g, carry, k=k, part=part, total=total):
                groups[part * GROUPS + total + g] = (k * ROOM + g * JOIN) | ((k % OWN) << 16)
                return carry

            lax.fori_loop(0, several, enter, 0)
            total = total + several
        for w in range(WIDE):
            groups[part * GROUPS + total + w] = LISTS * ROOM
        sizes[part] = (total + (WIDE - 1)) // WIDE


def plan(table, src, operand, count):
    return pl.pallas_call(
        plan_kernel,
        out_shape=(
            jax.ShapeDtypeStruct(((LISTS + 1) * ROOM,), jnp.int32),
            jax.ShapeDtypeStruct((2 * GROUPS,), jnp.int32),
            jax.ShapeDtypeStruct((2,), jnp.int32),
        ),
        in_specs=[SMEM] * 4,
        out_specs=(SMEM,) * 3,
        scratch_shapes=[pltpu.SMEM((LISTS,), jnp.int32)],
        cost_estimate=pl.CostEstimate(flops=5_000_000_000, bytes_accessed=16384, transcendentals=0),
        compiler_params=LIMIT,
        name="plan",
    )(table, src, operand, count)


def add_pairs(part, lists, groups, sizes, blocks, sources, total):
    def step(i, carry):
        made = []
        for w in range(WIDE):
            group = groups[part * GROUPS + i * WIDE + w]
            base = group & 0xFFFF
            left, right = [], []
            for u in range(JOIN):
                word = lists[base + u]
                left.append(blocks[(word >> 8) & 0x7F])
                right.append(sources[word & 0xFF])
            product = jnp.dot(
                jnp.concatenate(left, axis=1),
                jnp.concatenate(right, axis=0),
                preferred_element_type=jnp.float32,
            )
            made.append((group >> 16, product))
        for target, product in made:
            total[target] += product
        return carry

    lax.fori_loop(0, sizes[part], step, 0)


def fetch(pieces, places, sources, sems):
    copies = []
    for n, (piece, place) in enumerate(zip(pieces, places)):
        copy = pltpu.make_async_copy(piece, sources.at[pl.ds(place, piece.shape[0])], sems.at[n])
        copy.start()
        copies.append(copy)
    sources[SOURCES] = jnp.zeros((TILE, TILE), jnp.bfloat16)
    for copy in copies:
        copy.wait()


def early_kernel(lists, groups, sizes, blocks, incident, *rest):
    pieces, (total, sources, sems) = rest[:-3], rest[-3:]
    fetch(pieces, EARLY_AT, sources, sems)
    total[...] = incident[...].astype(jnp.float32)
    add_pairs(0, lists, groups, sizes, blocks, sources, total)


def finish(tmatrix, total, t):
    field = total[t].astype(jnp.bfloat16)
    return jnp.dot(tmatrix[t], field, preferred_element_type=jnp.float32).astype(jnp.bfloat16)


def late_kernel(lists, groups, sizes, blocks, before, tmatrix, *rest):
    pieces, (coeff, sources, total, sems) = rest[:-4], rest[-4:]
    fetch(pieces, LATE_AT, sources, sems)
    total[...] = before[...]
    add_pairs(1, lists, groups, sizes, blocks, sources, total)
    for t in range(OWN):
        coeff[t] = finish(tmatrix, total, t)


FAR_ROWS = 256


def last_kernel(lists, groups, sizes, blocks, before, tmatrix, weighted_a, weighted_b, *rest):
    pieces, (far, sources, total, coeff, sems) = rest[:-5], rest[-5:]
    fetch(pieces, LATE_AT, sources, sems)
    total[...] = before[...]
    add_pairs(1, lists, groups, sizes, blocks, sources, total)
    for t in range(OWN):
        coeff[pl.ds(t * TILE, TILE), :] = finish(tmatrix, total, t)

    for n, weighted in enumerate((weighted_a, weighted_b)):
        size = weighted.shape[0]

        def chunk(i, carry, weighted=weighted, first=n * size):
            start = pl.multiple_of(i * FAR_ROWS, FAR_ROWS)
            far[pl.ds(first + start, FAR_ROWS), :] = jnp.dot(
                weighted[pl.ds(start, FAR_ROWS), :],
                coeff[...],
                preferred_element_type=jnp.float32,
            )
            return carry

        lax.fori_loop(0, size // FAR_ROWS, chunk, 0)


def table_kernel(phases, harmonics, table):
    def chunk(i, carry):
        rows = pl.ds(pl.multiple_of(i * FAR_ROWS, FAR_ROWS), FAR_ROWS)
        modes = harmonics[rows, :].astype(jnp.float32)
        for s in range(OWN):
            phase = jnp.broadcast_to(phases[rows, s : s + 1], modes.shape)
            table[rows, s * TILE : (s + 1) * TILE] = (phase * modes).astype(jnp.bfloat16)
        return carry

    lax.fori_loop(0, table.shape[0] // FAR_ROWS, chunk, 0)


def order_kernel(order, table, ordered):
    def chunk(i, carry):
        rows = pl.ds(pl.multiple_of(i * FAR_ROWS, FAR_ROWS), FAR_ROWS)
        wanted = jnp.broadcast_to(order[rows, :], (FAR_ROWS, table.shape[0]))
        place = lax.broadcasted_iota(jnp.int32, wanted.shape, 1)
        pick = jnp.where(wanted == place, 1.0, 0.0).astype(jnp.bfloat16)
        ordered[rows, :] = jnp.dot(pick, table[...], preferred_element_type=jnp.float32).astype(
            jnp.bfloat16
        )
        return carry

    lax.fori_loop(0, ordered.shape[0] // FAR_ROWS, chunk, 0)


def make_table(factor, harmonics):
    return pl.pallas_call(
        table_kernel,
        out_shape=jax.ShapeDtypeStruct((harmonics.shape[0], OWN * TILE), jnp.bfloat16),
        in_specs=[VMEM] * 2,
        out_specs=VMEM,
        compiler_params=LIMIT,
        cost_estimate=pl.CostEstimate(
            flops=1_000_000_000, bytes_accessed=4_000_000, transcendentals=0
        ),
        name="table",
    )(factor.T, harmonics)


def in_order(order, table):
    return pl.pallas_call(
        order_kernel,
        out_shape=jax.ShapeDtypeStruct((order.shape[0], OWN * TILE), jnp.bfloat16),
        in_specs=[VMEM] * 2,
        out_specs=VMEM,
        compiler_params=LIMIT,
        cost_estimate=pl.CostEstimate(
            flops=2_000_000_000, bytes_accessed=4_000_000, transcendentals=0
        ),
        name="order",
    )(order[:, None], table)


SCRATCH = pltpu.VMEM((SOURCES + 1, TILE, TILE), jnp.bfloat16)
TOTAL = (OWN, TILE, TILE)


def early_pairs(made, blocks, incident, pieces):
    return pl.pallas_call(
        early_kernel,
        out_shape=jax.ShapeDtypeStruct(TOTAL, jnp.float32),
        in_specs=[SMEM] * 3 + [VMEM] * 2 + [ANY] * len(pieces),
        out_specs=VMEM,
        scratch_shapes=[SCRATCH, pltpu.SemaphoreType.DMA((len(pieces),))],
        cost_estimate=pl.CostEstimate(
            flops=2_000_000_000, bytes_accessed=8_000_000, transcendentals=0
        ),
        compiler_params=LIMIT,
        name="early",
    )(*made, blocks, incident, *pieces)


def late_pairs(made, blocks, before, tmatrix, pieces):
    return pl.pallas_call(
        late_kernel,
        out_shape=jax.ShapeDtypeStruct(TOTAL, jnp.bfloat16),
        in_specs=[SMEM] * 3 + [VMEM] * 3 + [ANY] * len(pieces),
        out_specs=VMEM,
        scratch_shapes=[
            SCRATCH,
            pltpu.VMEM(TOTAL, jnp.float32),
            pltpu.SemaphoreType.DMA((len(pieces),)),
        ],
        compiler_params=LIMIT,
        name="late",
    )(*made, blocks, before, tmatrix, *pieces)


def last_pairs(made, blocks, before, tmatrix, weighted, pieces):
    rows = sum(part.shape[0] for part in weighted)
    return pl.pallas_call(
        last_kernel,
        out_shape=jax.ShapeDtypeStruct((rows, TILE), jnp.float32),
        in_specs=[SMEM] * 3 + [VMEM] * 5 + [ANY] * len(pieces),
        out_specs=VMEM,
        scratch_shapes=[
            SCRATCH,
            pltpu.VMEM(TOTAL, jnp.float32),
            pltpu.VMEM((OWN * TILE, TILE), jnp.bfloat16),
            pltpu.SemaphoreType.DMA((len(pieces),)),
        ],
        compiler_params=LIMIT,
        name="last",
    )(*made, blocks, before, tmatrix, *weighted, *pieces)


def apply_tmatrix(tmatrix, field):
    product = jnp.einsum("skl,slq->skq", tmatrix, field, preferred_element_type=jnp.float32)
    return product.astype(jnp.bfloat16)


def body(
    incident,
    tmatrix,
    blocks,
    need,
    pair_src,
    pair_tgt,
    pair_blk,
    pair_count,
    factor,
    harmonics,
    owner,
):
    n_grp, n_dev = lax.axis_size("grp"), lax.axis_size("dev")
    coeff = apply_tmatrix(tmatrix, incident)
    made = plan(source_table(need[0]), pair_src[0], pair_tgt[0] | (pair_blk[0] << 8), pair_count)
    table = make_table(factor, harmonics)
    near, other, far = spread(coeff, table, made)
    before = early_pairs(made, blocks, incident, near + other)
    coeff = late_pairs(made, blocks, before, tmatrix, swapped(far, before))

    rows = owner.shape[0] // (n_grp * n_dev)
    order = owner.reshape(n_grp, n_dev, rows).transpose(1, 0, 2).reshape(2, -1)
    weighted = tuple(in_order(part, table) for part in order)
    near, other, far = spread(coeff, weighted[0], weighted[1])
    before = early_pairs(made, blocks, incident, near + other)
    far = last_pairs(made, blocks, before, tmatrix, weighted, swapped(far, before))

    far = far.reshape(n_dev, n_grp * rows, TILE)
    far = lax.all_to_all(far, "dev", 0, 0).sum(axis=0)
    far = far.reshape(n_grp, rows, TILE)
    return lax.all_to_all(far, "grp", 0, 0).sum(axis=0)


def solution(mesh):
    both = ("grp", "dev")
    return jax.shard_map(
        body,
        mesh=mesh,
        in_specs=(
            P(both, None, None),
            P(both, None, None),
            P(both, None, None),
            P(both, None, None),
            P(both, None),
            P(both, None),
            P(both, None),
            P(both),
            P(both, None),
            P(),
            P(),
        ),
        out_specs=P(both, None),
        check_vma=False,
    )
```

```python
import jax
import jax.numpy as jnp
from jax import lax
from jax.experimental import pallas as pl
from jax.experimental.pallas import tpu as pltpu
from jax.sharding import PartitionSpec as P

SIDE = 4
OWN = 4
SOURCES = 2 * SIDE * SIDE * OWN
BLOCKS = 128
PAIRS = 512
TILE = 128
JOIN = 8
WIDE = 4
LATE_GROUP = 72
GROUPS = 2 * LATE_GROUP

LIMIT = pltpu.CompilerParams(vmem_limit_bytes=16 << 20)
SMEM = pl.BlockSpec(memory_space=pltpu.SMEM)
VMEM = pl.BlockSpec(memory_space=pltpu.VMEM)
ANY = pl.BlockSpec(memory_space=pl.ANY)


def device_of(x, y, core):
    return ((x % SIDE) * SIDE + y % SIDE) * 2 + core


def moves(step):
    spots = [(x, y, c) for x in range(SIDE) for y in range(SIDE) for c in range(2)]
    return [(device_of(*spot), device_of(*step(*spot))) for spot in spots]


def along_first(shift):
    return moves(lambda x, y, c: (x + shift, y, c) if c == 0 else (x, y + shift, c))


def along_second(shift):
    return moves(lambda x, y, c: (x, y + shift, c) if c == 0 else (x + shift, y, c))


SWAP = moves(lambda x, y, c: (x, y, 1 - c))
SAME_CORE = [[device_of(x, y, c) for x in range(SIDE) for y in range(SIDE)] for c in range(2)]


def send(values, pairs):
    return lax.ppermute(values, "dev", pairs)


def together(values, *fillers):
    return lax.optimization_barrier((values, fillers))[0]


def spread(coeff, fill_first, fill_second):
    first2 = send(coeff, along_first(2))
    first3 = send(coeff, along_first(1))
    first1 = send(coeff, along_first(-1))
    first2, first3, first1 = together((first2, first3, first1), *fill_first)
    low = jnp.concatenate([coeff, first1])
    high = jnp.concatenate([first2, first3])
    low3 = send(low, along_second(1))
    high1 = send(high, along_second(-1))
    high3 = send(high, along_second(1))
    low1 = send(low, along_second(-1))
    low2 = send(low3, along_second(1))
    high2 = send(high1, along_second(-1))
    high3, low1 = together((high3, low1), *fill_second)
    near = (low, high, low1, high1, low3, high3)
    far = (low2, high2)
    return near, tuple(send(piece, SWAP) for piece in near), far


def swapped(pieces, before):
    pieces = together(pieces, before)
    return pieces + tuple(send(piece, SWAP) for piece in pieces)


NEAR_AT = (0, 8, 16, 24, 48, 56)
FAR_AT = (32, 40)
EARLY_AT = NEAR_AT + tuple(place + SOURCES // 2 for place in NEAR_AT)
LATE_AT = FAR_AT + tuple(place + SOURCES // 2 for place in FAR_AT)


def ones_where(mask):
    return jnp.where(mask, 1.0, 0.0).astype(jnp.bfloat16)


def counted(shape, axis):
    return lax.broadcasted_iota(jnp.int32, shape, axis)


def dot(left, right, contract=((1,), (0,))):
    return lax.dot_general(left, right, (contract, ((), ())), preferred_element_type=jnp.float32)


def plan_kernel(me, count, need, src, tgt, blk, blocks, words, groups, sizes, near, sem):
    copy = pltpu.make_async_copy(blocks, near, sem)
    copy.start()
    source = src[...]
    peer, request = source >> 2, source & 3
    from_peer = ones_where(counted((need.shape[0], PAIRS), 0) == peer)
    choices = dot(need[...].astype(jnp.float32).astype(jnp.bfloat16), from_peer, ((0,), (0,)))
    sphere = jnp.zeros((1, PAIRS), jnp.float32)
    for k in range(OWN):
        sphere = jnp.where(request == k, choices[k : k + 1, :], sphere)
    core = peer & 1
    dx = ((peer >> 3) - (me[0] >> 3)) & 3
    dy = (((peer >> 1) & 3) - ((me[0] >> 1) & 3)) & 3
    first = jnp.where(core == 0, dx, dy)
    second = jnp.where(core == 0, dy, dx)
    slot = ((core ^ (me[0] & 1)) << 6) + (second << 4) + (first << 2) + sphere.astype(jnp.int32)
    which = tgt[...] + jnp.where(second == 2, OWN, 0)
    live = counted((1, PAIRS), 1) < count[0]

    rows = 16
    row = counted((rows, PAIRS), 0)
    member = (row == which) & live
    ahead = ones_where(counted((PAIRS, PAIRS), 0) < counted((PAIRS, PAIRS), 1))
    rank = dot(ones_where(member), ahead)
    many = jnp.sum(jnp.where(member, 1.0, 0.0), axis=1, keepdims=True).astype(jnp.int32)
    several = (many + (JOIN - 1)) // JOIN
    r, c = counted((rows, rows), 0), counted((rows, rows), 1)
    below = ones_where((c < r) & ((c < OWN) == (r < OWN)))
    wide = jnp.broadcast_to(several, (rows, TILE)).astype(jnp.float32).astype(jnp.bfloat16)
    begin = dot(below, wide)[:, :1].astype(jnp.int32)
    begin = begin + jnp.where(counted((rows, 1), 0) < OWN, 0, LATE_GROUP)

    at = rank.astype(jnp.int32) + begin * JOIN
    at = jnp.sum(jnp.where(member, at, 0).astype(jnp.float32), axis=0, keepdims=True)
    at = jnp.where(live, at.astype(jnp.int32), -1)
    placed = ones_where(counted((GROUPS * JOIN, PAIRS), 0) == at)
    values = jnp.where(row == 0, slot - SOURCES, jnp.where(row == 1, blk[...], 0))
    values = values.astype(jnp.float32).astype(jnp.bfloat16)
    listed = dot(values, placed, ((1,), (1,))).astype(jnp.int32)
    words[...] = (listed[0:1, :] + SOURCES) | (listed[1:2, :] << 8)

    group = counted((rows, 2 * TILE), 1)
    passed = (group >= begin) & (counted((rows, 2 * TILE), 0) < 2 * OWN)
    owner = jnp.sum(jnp.where(passed, 1.0, 0.0), axis=0, keepdims=True).astype(jnp.int32) - 1
    groups[...] = (group[0:1, :] * JOIN) | ((owner & (OWN - 1)) << 16)

    lane = counted((1, TILE), 1)
    part = counted((rows, 1), 0) // OWN
    steps = jnp.zeros((1, TILE), jnp.int32)
    for k in range(2):
        total = jnp.sum(jnp.where(part == k, several, 0).astype(jnp.float32), axis=0, keepdims=True)
        needed = (total.astype(jnp.int32) + (WIDE - 1)) // WIDE
        steps = jnp.where(lane == k, needed, steps)
    sizes[...] = steps
    copy.wait()


def plan(need, src, tgt, blk, count, blocks):
    me = lax.axis_index("dev").reshape(1)
    words, groups, sizes, near = pl.pallas_call(
        plan_kernel,
        out_shape=(
            jax.ShapeDtypeStruct((1, GROUPS * JOIN), jnp.int32),
            jax.ShapeDtypeStruct((1, 2 * TILE), jnp.int32),
            jax.ShapeDtypeStruct((1, TILE), jnp.int32),
            jax.ShapeDtypeStruct(blocks.shape, blocks.dtype),
        ),
        in_specs=[SMEM] * 2 + [VMEM] * 4 + [ANY],
        out_specs=(VMEM,) * 4,
        scratch_shapes=[pltpu.SemaphoreType.DMA],
        compiler_params=LIMIT,
        cost_estimate=pl.CostEstimate(
            flops=1_000_000_000, bytes_accessed=8_000_000, transcendentals=0
        ),
        name="plan",
    )(me, count, need, src, tgt, blk, blocks)
    return (words, groups, sizes), near


def add_pairs(part, lists, groups, sizes, blocks, sources, total):
    def step(i, carry):
        made = []
        for w in range(WIDE):
            group = groups[0, part * LATE_GROUP + i * WIDE + w]
            base = group & 0xFFFF
            left, right = [], []
            for u in range(JOIN):
                word = lists[0, base + u]
                left.append(blocks[word >> 8])
                right.append(sources[word & 0xFF])
            product = jnp.dot(
                jnp.concatenate(left, axis=1),
                jnp.concatenate(right, axis=0),
                preferred_element_type=jnp.float32,
            )
            made.append((group >> 16, product))
        for target, product in made:
            total[target] += product
        return carry

    lax.fori_loop(0, sizes[0, part], step, 0)


def fetch(pieces, places, sources, sems):
    copies = []
    for n, (piece, place) in enumerate(zip(pieces, places)):
        copy = pltpu.make_async_copy(piece, sources.at[pl.ds(place, piece.shape[0])], sems.at[n])
        copy.start()
        copies.append(copy)
    sources[SOURCES] = jnp.zeros((TILE, TILE), jnp.bfloat16)
    for copy in copies:
        copy.wait()


def early_kernel(lists, groups, sizes, blocks, incident, *rest):
    pieces, (total, sources, sems) = rest[:-3], rest[-3:]
    fetch(pieces, EARLY_AT, sources, sems)
    total[...] = incident[...].astype(jnp.float32)
    add_pairs(0, lists, groups, sizes, blocks, sources, total)


def finish(tmatrix, total, t):
    field = total[t].astype(jnp.bfloat16)
    return jnp.dot(tmatrix[t], field, preferred_element_type=jnp.float32).astype(jnp.bfloat16)


def late_kernel(lists, groups, sizes, blocks, before, tmatrix, *rest):
    pieces, (coeff, sources, total, sems) = rest[:-4], rest[-4:]
    fetch(pieces, LATE_AT, sources, sems)
    total[...] = before[...]
    add_pairs(1, lists, groups, sizes, blocks, sources, total)
    for t in range(OWN):
        coeff[t] = finish(tmatrix, total, t)


FAR_ROWS = 256


def far_kernel(mine, other, coeff, arrived, far):
    def chunk(i, carry):
        rows = pl.ds(pl.multiple_of(i * FAR_ROWS, FAR_ROWS), FAR_ROWS)
        far[rows, :] = dot(mine[rows, :], coeff[...]) + dot(other[rows, :], arrived[...])
        return carry

    lax.fori_loop(0, far.shape[0] // FAR_ROWS, chunk, 0)


def far_field(mine, other, coeff, arrived):
    return pl.pallas_call(
        far_kernel,
        out_shape=jax.ShapeDtypeStruct((mine.shape[0], TILE), jnp.float32),
        in_specs=[VMEM] * 4,
        out_specs=VMEM,
        compiler_params=LIMIT,
        name="far",
    )(mine, other, coeff.reshape(-1, TILE), arrived.reshape(-1, TILE))


def table_kernel(phases, harmonics, table):
    def chunk(i, carry):
        rows = pl.ds(pl.multiple_of(i * FAR_ROWS, FAR_ROWS), FAR_ROWS)
        modes = harmonics[rows, :].astype(jnp.float32)
        for s in range(OWN):
            phase = jnp.broadcast_to(phases[rows, s : s + 1], modes.shape)
            table[rows, s * TILE : (s + 1) * TILE] = (phase * modes).astype(jnp.bfloat16)
        return carry

    lax.fori_loop(0, table.shape[0] // FAR_ROWS, chunk, 0)


def order_kernel(order, table, ordered):
    def chunk(i, carry):
        rows = pl.ds(pl.multiple_of(i * FAR_ROWS, FAR_ROWS), FAR_ROWS)
        wanted = jnp.broadcast_to(order[rows, :], (FAR_ROWS, table.shape[0]))
        place = lax.broadcasted_iota(jnp.int32, wanted.shape, 1)
        pick = jnp.where(wanted == place, 1.0, 0.0).astype(jnp.bfloat16)
        ordered[rows, :] = jnp.dot(pick, table[...], preferred_element_type=jnp.float32).astype(
            jnp.bfloat16
        )
        return carry

    lax.fori_loop(0, ordered.shape[0] // FAR_ROWS, chunk, 0)


def make_table(factor, harmonics):
    return pl.pallas_call(
        table_kernel,
        out_shape=jax.ShapeDtypeStruct((harmonics.shape[0], OWN * TILE), jnp.bfloat16),
        in_specs=[VMEM] * 2,
        out_specs=VMEM,
        compiler_params=LIMIT,
        cost_estimate=pl.CostEstimate(
            flops=1_000_000_000, bytes_accessed=4_000_000, transcendentals=0
        ),
        name="table",
    )(factor.T, harmonics)


def in_order(order, table):
    return pl.pallas_call(
        order_kernel,
        out_shape=jax.ShapeDtypeStruct((order.shape[0], OWN * TILE), jnp.bfloat16),
        in_specs=[VMEM] * 2,
        out_specs=VMEM,
        compiler_params=LIMIT,
        cost_estimate=pl.CostEstimate(
            flops=2_000_000_000, bytes_accessed=4_000_000, transcendentals=0
        ),
        name="order",
    )(order[:, None], table)


SCRATCH = pltpu.VMEM((SOURCES + 1, TILE, TILE), jnp.bfloat16)
TOTAL = (OWN, TILE, TILE)


def early_pairs(made, blocks, incident, pieces):
    return pl.pallas_call(
        early_kernel,
        out_shape=jax.ShapeDtypeStruct(TOTAL, jnp.float32),
        in_specs=[SMEM] * 3 + [VMEM] * 2 + [ANY] * len(pieces),
        out_specs=VMEM,
        scratch_shapes=[SCRATCH, pltpu.SemaphoreType.DMA((len(pieces),))],
        cost_estimate=pl.CostEstimate(
            flops=2_000_000_000, bytes_accessed=8_000_000, transcendentals=0
        ),
        compiler_params=LIMIT,
        name="early",
    )(*made, blocks, incident, *pieces)


def late_pairs(made, blocks, before, tmatrix, pieces):
    return pl.pallas_call(
        late_kernel,
        out_shape=jax.ShapeDtypeStruct(TOTAL, jnp.bfloat16),
        in_specs=[SMEM] * 3 + [VMEM] * 3 + [ANY] * len(pieces),
        out_specs=VMEM,
        scratch_shapes=[
            SCRATCH,
            pltpu.VMEM(TOTAL, jnp.float32),
            pltpu.SemaphoreType.DMA((len(pieces),)),
        ],
        compiler_params=LIMIT,
        name="late",
    )(*made, blocks, before, tmatrix, *pieces)


def apply_tmatrix(tmatrix, field):
    product = jnp.einsum("skl,slq->skq", tmatrix, field, preferred_element_type=jnp.float32)
    return product.astype(jnp.bfloat16)


def body(
    incident,
    tmatrix,
    blocks,
    need,
    pair_src,
    pair_tgt,
    pair_blk,
    pair_count,
    factor,
    harmonics,
    owner,
):
    n_grp, n_dev = lax.axis_size("grp"), lax.axis_size("dev")
    coeff = apply_tmatrix(tmatrix, incident)
    made, blocks = plan(need[0], pair_src, pair_tgt, pair_blk, pair_count, blocks)
    table = make_table(factor, harmonics)

    rows = owner.shape[0] // (n_grp * n_dev)
    order = owner.reshape(n_grp, n_dev // 2, 2, rows).transpose(2, 1, 0, 3).reshape(2, -1)
    core = lax.axis_index("dev") % 2
    order_mine = jnp.where(core == 0, order[0], order[1])
    order_other = jnp.where(core == 0, order[1], order[0])
    for_other = in_order(order_other, table)
    near, other, far = spread(coeff, (made, table), (for_other,))
    before = early_pairs(made, blocks, incident, near + other)
    coeff = late_pairs(made, blocks, before, tmatrix, swapped(far, before))

    mine = in_order(order_mine, table)
    near, other, far = spread(coeff, (mine,), ())
    weighted_other = send(for_other, SWAP)
    before = early_pairs(made, blocks, incident, near + other)
    coeff = late_pairs(made, blocks, before, tmatrix, swapped(far, before))

    amplitude = far_field(mine, weighted_other, coeff, send(coeff, SWAP))
    amplitude = amplitude.reshape(n_dev // 2, n_grp * rows, TILE)
    amplitude = lax.all_to_all(amplitude, "dev", 0, 0, axis_index_groups=SAME_CORE).sum(axis=0)
    amplitude = amplitude.reshape(n_grp, rows, TILE)
    return lax.all_to_all(amplitude, "grp", 0, 0).sum(axis=0)


def solution(mesh):
    both = ("grp", "dev")
    return jax.shard_map(
        body,
        mesh=mesh,
        in_specs=(
            P(both, None, None),
            P(both, None, None),
            P(both, None, None),
            P(both, None, None),
            P(both, None),
            P(both, None),
            P(both, None),
            P(both),
            P(both, None),
            P(),
            P(),
        ),
        out_specs=P(both, None),
        check_vma=False,
    )
```

```python
import jax
import jax.numpy as jnp
from jax import lax
from jax.experimental import pallas as pl
from jax.experimental.pallas import tpu as pltpu
from jax.sharding import PartitionSpec as P


SIDE = 4
OWN = 4
SOURCES = 2 * SIDE * SIDE * OWN
PAIRS = 512
TILE = 128
JOIN = 8
WIDE = 4
LATE_GROUP = 72
GROUPS = 2 * LATE_GROUP

LIMIT = pltpu.CompilerParams(vmem_limit_bytes=16 << 20)
SMEM = pl.BlockSpec(memory_space=pltpu.SMEM)
VMEM = pl.BlockSpec(memory_space=pltpu.VMEM)
ANY = pl.BlockSpec(memory_space=pl.ANY)
HBM = pl.BlockSpec(memory_space=pltpu.HBM)


def device_of(x, y, core):
    return ((x % SIDE) * SIDE + y % SIDE) * 2 + core


def moves(step):
    spots = [(x, y, c) for x in range(SIDE) for y in range(SIDE) for c in range(2)]
    return [(device_of(*spot), device_of(*step(*spot))) for spot in spots]


def along_first(shift):
    return moves(lambda x, y, c: (x + shift, y, c) if c == 0 else (x, y + shift, c))


def along_second(shift):
    return moves(lambda x, y, c: (x, y + shift, c) if c == 0 else (x + shift, y, c))


SWAP = moves(lambda x, y, c: (x, y, 1 - c))
SAME_CORE = [[device_of(x, y, c) for x in range(SIDE) for y in range(SIDE)] for c in range(2)]


def send(values, pairs):
    return lax.ppermute(values, "dev", pairs)


def stay(values):
    return pltpu.with_memory_space_constraint(values, pltpu.HBM)


def together(values, *fillers):
    return lax.optimization_barrier((values, fillers))[0]


def spread(coeff, *fillers):
    first2 = send(coeff, along_first(2))
    first3 = send(coeff, along_first(1))
    first1 = send(coeff, along_first(-1))
    first2, first3, first1 = together((first2, first3, first1), *fillers)
    low = jnp.concatenate([coeff, first1])
    high = jnp.concatenate([first2, first3])
    low3 = send(low, along_second(1))
    high1 = send(high, along_second(-1))
    high3 = send(high, along_second(1))
    low1 = send(low, along_second(-1))
    low2 = send(low3, along_second(1))
    high2 = send(high1, along_second(-1))
    near = (low, high, low1, high1, low3, high3)
    other = (send(low, SWAP), send(high, SWAP))
    other += tuple(send(piece, SWAP) for piece in near[2:])
    return near, other, (low2, high2)


def swapped(pieces, before):
    pieces = together(pieces, before)
    return pieces + tuple(send(piece, SWAP) for piece in pieces)


NEAR_AT = (0, 8, 16, 24, 48, 56)
FAR_AT = (32, 40)
EARLY_AT = NEAR_AT + tuple(place + SOURCES // 2 for place in NEAR_AT)
LATE_AT = FAR_AT + tuple(place + SOURCES // 2 for place in FAR_AT)


def ones_where(mask):
    return jnp.where(mask, 1.0, 0.0).astype(jnp.bfloat16)


def counted(shape, axis):
    return lax.broadcasted_iota(jnp.int32, shape, axis)


def dot(left, right, contract=((1,), (0,))):
    return lax.dot_general(left, right, (contract, ((), ())), preferred_element_type=jnp.float32)


def plan_kernel(me, count, need, src, tgt, blk, words, groups, sizes):
    source = src[...]
    peer, request = source >> 2, source & 3
    from_peer = ones_where(counted((need.shape[0], PAIRS), 0) == peer)
    choices = dot(need[...].astype(jnp.float32).astype(jnp.bfloat16), from_peer, ((0,), (0,)))
    sphere = jnp.zeros((1, PAIRS), jnp.float32)
    for k in range(OWN):
        sphere = jnp.where(request == k, choices[k : k + 1, :], sphere)
    core = peer & 1
    dx = ((peer >> 3) - (me[0] >> 3)) & 3
    dy = (((peer >> 1) & 3) - ((me[0] >> 1) & 3)) & 3
    first = jnp.where(core == 0, dx, dy)
    second = jnp.where(core == 0, dy, dx)
    slot = ((core ^ (me[0] & 1)) << 6) + (second << 4) + (first << 2) + sphere.astype(jnp.int32)
    which = tgt[...] + jnp.where(second == 2, OWN, 0)
    live = counted((1, PAIRS), 1) < count[0]

    rows = 16
    row = counted((rows, PAIRS), 0)
    member = (row == which) & live
    ahead = ones_where(counted((PAIRS, PAIRS), 0) < counted((PAIRS, PAIRS), 1))
    rank = dot(ones_where(member), ahead)
    many = jnp.sum(jnp.where(member, 1.0, 0.0), axis=1, keepdims=True).astype(jnp.int32)
    several = (many + (JOIN - 1)) // JOIN
    r, c = counted((rows, rows), 0), counted((rows, rows), 1)
    below = ones_where((c < r) & ((c < OWN) == (r < OWN)))
    wide = jnp.broadcast_to(several, (rows, TILE)).astype(jnp.float32).astype(jnp.bfloat16)
    begin = dot(below, wide)[:, :1].astype(jnp.int32)
    begin = begin + jnp.where(counted((rows, 1), 0) < OWN, 0, LATE_GROUP)

    at = rank.astype(jnp.int32) + begin * JOIN
    at = jnp.sum(jnp.where(member, at, 0).astype(jnp.float32), axis=0, keepdims=True)
    at = jnp.where(live, at.astype(jnp.int32), -1)
    placed = ones_where(counted((GROUPS * JOIN, PAIRS), 0) == at)
    values = jnp.where(row == 0, slot - SOURCES, jnp.where(row == 1, blk[...], 0))
    values = values.astype(jnp.float32).astype(jnp.bfloat16)
    listed = dot(values, placed, ((1,), (1,))).astype(jnp.int32)
    words[...] = (listed[0:1, :] + SOURCES) | (listed[1:2, :] << 8)

    group = counted((rows, 2 * TILE), 1)
    passed = (group >= begin) & (counted((rows, 2 * TILE), 0) < 2 * OWN)
    owner = jnp.sum(jnp.where(passed, 1.0, 0.0), axis=0, keepdims=True).astype(jnp.int32) - 1
    groups[...] = (group[0:1, :] * JOIN) | ((owner & (OWN - 1)) << 16)

    lane = counted((1, TILE), 1)
    part = counted((rows, 1), 0) // OWN
    steps = jnp.zeros((1, TILE), jnp.int32)
    for k in range(2):
        total = jnp.sum(jnp.where(part == k, several, 0).astype(jnp.float32), axis=0, keepdims=True)
        needed = (total.astype(jnp.int32) + (WIDE - 1)) // WIDE
        steps = jnp.where(lane == k, needed, steps)
    sizes[...] = steps


def plan(need, src, tgt, blk, count):
    me = lax.axis_index("dev").reshape(1)
    return pl.pallas_call(
        plan_kernel,
        out_shape=(
            jax.ShapeDtypeStruct((1, GROUPS * JOIN), jnp.int32),
            jax.ShapeDtypeStruct((1, 2 * TILE), jnp.int32),
            jax.ShapeDtypeStruct((1, TILE), jnp.int32),
        ),
        in_specs=[SMEM] * 2 + [VMEM] * 4,
        out_specs=(VMEM,) * 3,
        compiler_params=LIMIT,
        cost_estimate=pl.CostEstimate(
            flops=1_000_000_000, bytes_accessed=1_000_000, transcendentals=0
        ),
        name="plan",
    )(me, count, need, src, tgt, blk)


def add_pairs(part, lists, groups, sizes, blocks, sources, total):
    def several(count, first):
        made = []
        for w in range(count):
            group = groups[0, part * LATE_GROUP + first + w]
            base = group & 0xFFFF
            left, right = [], []
            for u in range(JOIN):
                word = lists[0, base + u]
                left.append(blocks[word >> 8])
                right.append(sources[word & 0xFF])
            made.append((group >> 16, dot(jnp.concatenate(left, 1), jnp.concatenate(right, 0))))
        for target, product in made:
            total[target] += product

    def full(i, carry):
        several(2 * WIDE, i * (2 * WIDE))
        return carry

    def rest(i, carry):
        several(WIDE, i * WIDE)
        return carry

    steps = sizes[0, part]
    lax.fori_loop(0, steps // 2, full, 0)
    lax.fori_loop(steps // 2 * 2, steps, rest, 0)


def fetch(pieces, places, sources, sems):
    copies = []
    for n, (piece, place) in enumerate(zip(pieces, places)):
        there = sources.at[pl.ds(place, piece.shape[0])]
        copies.append(pltpu.make_async_copy(piece, there, sems.at[n]))
    for copy in copies:
        copy.start()
    sources[SOURCES] = jnp.zeros((TILE, TILE), jnp.bfloat16)
    return copies


def early_kernel(lists, groups, sizes, blocks, incident, *rest):
    pieces, (total, sources, sems) = rest[:-3], rest[-3:]
    copies = fetch(pieces, EARLY_AT, sources, sems)
    total[...] = incident[...].astype(jnp.float32)
    for copy in copies:
        copy.wait()
    add_pairs(0, lists, groups, sizes, blocks, sources, total)


def finish(tmatrix, total, t):
    field = total[t].astype(jnp.bfloat16)
    return jnp.dot(tmatrix[t], field, preferred_element_type=jnp.float32).astype(jnp.bfloat16)


def late_kernel(lists, groups, sizes, blocks, before, tmatrix, *rest):
    pieces, (coeff, sources, total, sems) = rest[:-4], rest[-4:]
    copies = fetch(pieces, LATE_AT, sources, sems)
    total[...] = before[...]
    for copy in copies:
        copy.wait()
    add_pairs(1, lists, groups, sizes, blocks, sources, total)
    for t in range(OWN):
        coeff[t] = finish(tmatrix, total, t)


FAR_ROWS = 256


def far_kernel(mine, other, coeff, arrived, far):
    def chunk(i, carry):
        rows = pl.ds(pl.multiple_of(i * FAR_ROWS, FAR_ROWS), FAR_ROWS)
        made = dot(mine[rows, :], coeff[...]) + dot(other[rows, :], arrived[...])
        far[rows, :] = made.astype(far.dtype)
        return carry

    lax.fori_loop(0, far.shape[0] // FAR_ROWS, chunk, 0)


def far_field(mine, other, coeff, arrived):
    return pl.pallas_call(
        far_kernel,
        out_shape=jax.ShapeDtypeStruct((mine.shape[0], TILE), jnp.bfloat16),
        in_specs=[VMEM] * 4,
        out_specs=VMEM,
        compiler_params=LIMIT,
        name="far",
    )(mine, other, coeff.reshape(-1, TILE), arrived.reshape(-1, TILE))


def order_kernel(order, factor_far, harmonics, ordered, right, factor, sems):
    first = pltpu.make_async_copy(factor_far, factor, sems.at[0])
    first.start()
    copy = pltpu.make_async_copy(harmonics, right.at[:, pl.ds(0, TILE)], sems.at[1])
    copy.start()
    first.wait()
    for i in range(right.shape[0] // FAR_ROWS):
        rows = pl.ds(i * FAR_ROWS, FAR_ROWS)
        phase = factor[:, rows]
        high = phase.astype(jnp.bfloat16).astype(jnp.float32)
        middle = (phase - high).astype(jnp.bfloat16).astype(jnp.float32)
        parts = [high, middle, phase - high - middle, jnp.zeros_like(phase)]
        parts = jnp.concatenate(parts, axis=0).T
        parts = jnp.concatenate([parts, jnp.zeros((FAR_ROWS, TILE - 4 * OWN), jnp.float32)], axis=1)
        right[rows, TILE:] = parts.astype(jnp.bfloat16)
    copy.wait()

    def chunk(i, carry):
        rows = pl.ds(pl.multiple_of(i * FAR_ROWS, FAR_ROWS), FAR_ROWS)
        wanted = jnp.broadcast_to(order[rows, :], (FAR_ROWS, right.shape[0]))
        pick = ones_where(wanted == counted(wanted.shape, 1))
        found = dot(pick, right[...])
        mode, parts = found[:, :TILE], found[:, TILE:]
        for s in range(OWN):
            phase = parts[:, s : s + 1] + parts[:, OWN + s : OWN + s + 1]
            phase = phase + parts[:, 2 * OWN + s : 2 * OWN + s + 1]
            made = jnp.broadcast_to(phase, mode.shape) * mode
            ordered[rows, s * TILE : (s + 1) * TILE] = made.astype(jnp.bfloat16)
        return carry

    lax.fori_loop(0, ordered.shape[0] // FAR_ROWS, chunk, 0)


def in_order(order, factor, harmonics):
    return pl.pallas_call(
        order_kernel,
        out_shape=jax.ShapeDtypeStruct((order.shape[0], OWN * TILE), jnp.bfloat16),
        in_specs=[VMEM] + [HBM] * 2,
        out_specs=VMEM,
        scratch_shapes=[
            pltpu.VMEM((harmonics.shape[0], 2 * TILE), jnp.bfloat16),
            pltpu.VMEM(factor.shape, factor.dtype),
            pltpu.SemaphoreType.DMA((2,)),
        ],
        compiler_params=LIMIT,
        cost_estimate=pl.CostEstimate(
            flops=2_000_000_000, bytes_accessed=4_000_000, transcendentals=0
        ),
        name="order",
    )(order, stay(factor), stay(harmonics))


SCRATCH = pltpu.VMEM((SOURCES + 1, TILE, TILE), jnp.bfloat16)
TOTAL = (OWN, TILE, TILE)


def early_pairs(made, blocks, incident, pieces):
    return pl.pallas_call(
        early_kernel,
        out_shape=jax.ShapeDtypeStruct(TOTAL, jnp.float32),
        in_specs=[SMEM] * 3 + [VMEM] * 2 + [ANY] * len(pieces),
        out_specs=VMEM,
        scratch_shapes=[SCRATCH, pltpu.SemaphoreType.DMA((len(pieces),))],
        cost_estimate=pl.CostEstimate(
            flops=2_000_000_000, bytes_accessed=8_000_000, transcendentals=0
        ),
        compiler_params=LIMIT,
        name="early",
    )(*made, blocks, incident, *pieces)


def late_pairs(made, blocks, before, tmatrix, pieces):
    return pl.pallas_call(
        late_kernel,
        out_shape=jax.ShapeDtypeStruct(TOTAL, jnp.bfloat16),
        in_specs=[SMEM] * 3 + [VMEM] * 3 + [ANY] * len(pieces),
        out_specs=VMEM,
        scratch_shapes=[
            SCRATCH,
            pltpu.VMEM(TOTAL, jnp.float32),
            pltpu.SemaphoreType.DMA((len(pieces),)),
        ],
        compiler_params=LIMIT,
        name="late",
    )(*made, blocks, before, tmatrix, *pieces)


def apply_tmatrix(tmatrix, field):
    product = jnp.einsum("skl,slq->skq", tmatrix, field, preferred_element_type=jnp.float32)
    return product.astype(jnp.bfloat16)


def body(
    incident,
    tmatrix,
    blocks,
    need,
    pair_src,
    pair_tgt,
    pair_blk,
    pair_count,
    factor,
    harmonics,
    owner,
):
    n_grp, n_dev = lax.axis_size("grp"), lax.axis_size("dev")
    coeff = apply_tmatrix(tmatrix, incident)
    made = plan(need[0], pair_src, pair_tgt, pair_blk, pair_count)

    rows = owner.shape[0] // (n_grp * n_dev)
    order = owner.reshape(n_grp * n_dev // 2, 2, rows).transpose(1, 0, 2).reshape(2, -1)
    core = lax.axis_index("dev") % 2
    order_mine = jnp.where(core == 0, order[0], order[1])
    order_other = jnp.where(core == 0, order[1], order[0])
    order_mine, order_other = lax.optimization_barrier((order_mine[:, None], order_other[:, None]))
    for_other = in_order(order_other, factor, harmonics)
    near, other, far = spread(coeff, made, for_other)
    before = early_pairs(made, blocks, incident, near + other)
    coeff = late_pairs(made, blocks, before, tmatrix, swapped(far, before))

    mine = in_order(order_mine, factor, harmonics)
    near, other, far = spread(coeff, mine)
    weighted_other = send(for_other, SWAP)
    before = early_pairs(made, blocks, incident, near + other)
    coeff = late_pairs(made, blocks, before, tmatrix, swapped(far, before))

    amplitude = far_field(mine, weighted_other, coeff, send(coeff, SWAP))
    amplitude = amplitude.reshape(n_grp * n_dev // 2, rows, TILE)
    groups = [[g * n_dev + d for g in range(n_grp) for d in same] for same in SAME_CORE]
    amplitude = lax.all_to_all(amplitude, ("grp", "dev"), 0, 0, axis_index_groups=groups)
    return amplitude.astype(jnp.float32).sum(axis=0)


def solution(mesh):
    both = ("grp", "dev")
    return jax.shard_map(
        body,
        mesh=mesh,
        in_specs=(
            P(both, None, None),
            P(both, None, None),
            P(both, None, None),
            P(both, None, None),
            P(both, None),
            P(both, None),
            P(both, None),
            P(both),
            P(both, None),
            P(),
            P(),
        ),
        out_specs=P(both, None),
        check_vma=False,
    )
```

```python
import jax
import jax.numpy as jnp
from jax import lax
from jax.experimental import pallas as pl
from jax.experimental.pallas import tpu as pltpu
from jax.sharding import PartitionSpec as P


SIDE = 4
OWN = 4
SOURCES = 2 * SIDE * SIDE * OWN
PAIRS = 512
TILE = 128
JOIN = 8
WIDE = 4
LATE_GROUP = 72
GROUPS = 2 * LATE_GROUP

LIMIT = pltpu.CompilerParams(vmem_limit_bytes=16 << 20)
SMEM = pl.BlockSpec(memory_space=pltpu.SMEM)
VMEM = pl.BlockSpec(memory_space=pltpu.VMEM)
ANY = pl.BlockSpec(memory_space=pl.ANY)
HBM = pl.BlockSpec(memory_space=pltpu.HBM)


def device_of(x, y, core):
    return ((x % SIDE) * SIDE + y % SIDE) * 2 + core


def moves(step):
    spots = [(x, y, c) for x in range(SIDE) for y in range(SIDE) for c in range(2)]
    return [(device_of(*spot), device_of(*step(*spot))) for spot in spots]


def along_first(shift):
    return moves(lambda x, y, c: (x + shift, y, c) if c == 0 else (x, y + shift, c))


def along_second(shift):
    return moves(lambda x, y, c: (x, y + shift, c) if c == 0 else (x + shift, y, c))


SWAP = moves(lambda x, y, c: (x, y, 1 - c))
SAME_CORE = [[device_of(x, y, c) for x in range(SIDE) for y in range(SIDE)] for c in range(2)]


def send(values, pairs):
    return lax.ppermute(values, "dev", pairs)


def stay(values):
    return pltpu.with_memory_space_constraint(values, pltpu.HBM)


def together(values, *fillers):
    return lax.optimization_barrier((values, fillers))[0]


def spread(coeff, fill_first, fill_second):
    first2 = send(coeff, along_first(2))
    first3 = send(coeff, along_first(1))
    first1 = send(coeff, along_first(-1))
    first2, first3, first1 = together((first2, first3, first1), *fill_first)
    low = jnp.concatenate([coeff, first1])
    high = jnp.concatenate([first2, first3])
    low3 = send(low, along_second(1))
    high1 = send(high, along_second(-1))
    high3 = send(high, along_second(1))
    low1 = send(low, along_second(-1))
    low2 = send(low3, along_second(1))
    high2 = send(high1, along_second(-1))
    high3, low1 = together((high3, low1), *fill_second)
    near = (low, high, low1, high1, low3, high3)
    return near, tuple(send(piece, SWAP) for piece in near), (low2, high2)


def swapped(pieces, before):
    pieces = together(pieces, before)
    return pieces + tuple(send(piece, SWAP) for piece in pieces)


NEAR_AT = (0, 8, 16, 24, 48, 56)
FAR_AT = (32, 40)
EARLY_AT = NEAR_AT + tuple(place + SOURCES // 2 for place in NEAR_AT)
LATE_AT = FAR_AT + tuple(place + SOURCES // 2 for place in FAR_AT)


def ones_where(mask):
    return jnp.where(mask, 1.0, 0.0).astype(jnp.bfloat16)


def counted(shape, axis):
    return lax.broadcasted_iota(jnp.int32, shape, axis)


def dot(left, right, contract=((1,), (0,))):
    return lax.dot_general(left, right, (contract, ((), ())), preferred_element_type=jnp.float32)


def plan_kernel(me, count, need, src, tgt, blk, words, groups, sizes):
    source = src[...]
    peer, request = source >> 2, source & 3
    from_peer = ones_where(counted((need.shape[1], PAIRS), 0) == peer)
    choices = dot(need[...].astype(jnp.float32).astype(jnp.bfloat16), from_peer)
    sphere = jnp.zeros((1, PAIRS), jnp.float32)
    for k in range(OWN):
        sphere = jnp.where(request == k, choices[k : k + 1, :], sphere)
    core = peer & 1
    dx = ((peer >> 3) - (me[0] >> 3)) & 3
    dy = (((peer >> 1) & 3) - ((me[0] >> 1) & 3)) & 3
    first = jnp.where(core == 0, dx, dy)
    second = jnp.where(core == 0, dy, dx)
    slot = ((core ^ (me[0] & 1)) << 6) + (second << 4) + (first << 2) + sphere.astype(jnp.int32)
    which = tgt[...] + jnp.where(second == 2, OWN, 0)
    live = counted((1, PAIRS), 1) < count[0]

    rows = 16
    row = counted((rows, PAIRS), 0)
    member = (row == which) & live
    ahead = ones_where(counted((PAIRS, PAIRS), 0) < counted((PAIRS, PAIRS), 1))
    rank = dot(ones_where(member), ahead)
    many = jnp.sum(jnp.where(member, 1.0, 0.0), axis=1, keepdims=True).astype(jnp.int32)
    several = (many + (JOIN - 1)) // JOIN
    r, c = counted((rows, rows), 0), counted((rows, rows), 1)
    below = ones_where((c < r) & ((c < OWN) == (r < OWN)))
    wide = jnp.broadcast_to(several, (rows, TILE)).astype(jnp.float32).astype(jnp.bfloat16)
    begin = dot(below, wide)[:, :1].astype(jnp.int32)
    begin = begin + jnp.where(counted((rows, 1), 0) < OWN, 0, LATE_GROUP)

    at = rank.astype(jnp.int32) + begin * JOIN
    at = jnp.sum(jnp.where(member, at, 0).astype(jnp.float32), axis=0, keepdims=True)
    at = jnp.where(live, at.astype(jnp.int32), -1)
    placed = ones_where(counted((GROUPS * JOIN, PAIRS), 0) == at)
    values = jnp.where(row == 0, slot - SOURCES, jnp.where(row == 1, blk[...], 0))
    values = values.astype(jnp.float32).astype(jnp.bfloat16)
    listed = dot(values, placed, ((1,), (1,))).astype(jnp.int32)
    words[...] = (listed[0:1, :] + SOURCES) | (listed[1:2, :] << 8)

    group = counted((rows, 2 * TILE), 1)
    passed = (group >= begin) & (counted((rows, 2 * TILE), 0) < 2 * OWN)
    owner = jnp.sum(jnp.where(passed, 1.0, 0.0), axis=0, keepdims=True).astype(jnp.int32) - 1
    groups[...] = (group[0:1, :] * JOIN) | ((owner & (OWN - 1)) << 16)

    lane = counted((1, TILE), 1)
    part = counted((rows, 1), 0) // OWN
    steps = jnp.zeros((1, TILE), jnp.int32)
    for k in range(2):
        total = jnp.sum(jnp.where(part == k, several, 0).astype(jnp.float32), axis=0, keepdims=True)
        needed = (total.astype(jnp.int32) + (WIDE - 1)) // WIDE
        steps = jnp.where(lane == k, needed, steps)
    sizes[...] = steps


def plan(need, src, tgt, blk, count):
    me = lax.axis_index("dev").reshape(1)
    return pl.pallas_call(
        plan_kernel,
        out_shape=(
            jax.ShapeDtypeStruct((1, GROUPS * JOIN), jnp.int32),
            jax.ShapeDtypeStruct((1, 2 * TILE), jnp.int32),
            jax.ShapeDtypeStruct((1, TILE), jnp.int32),
        ),
        in_specs=[SMEM] * 2 + [VMEM] * 4,
        out_specs=(VMEM,) * 3,
        compiler_params=LIMIT,
        cost_estimate=pl.CostEstimate(
            flops=8_000_000_000, bytes_accessed=1_000_000, transcendentals=0
        ),
        name="plan",
    )(me, count, need, src, tgt, blk)


def add_pairs(part, lists, groups, sizes, blocks, sources, total):
    def several(count, first):
        made = []
        for w in range(count):
            group = groups[0, part * LATE_GROUP + first + w]
            base = group & 0xFFFF
            left, right = [], []
            for u in range(JOIN):
                word = lists[0, base + u]
                left.append(blocks[word >> 8])
                right.append(sources[word & 0xFF])
            made.append((group >> 16, dot(jnp.concatenate(left, 1), jnp.concatenate(right, 0))))
        for target, product in made:
            total[target] += product

    def full(i, carry):
        several(2 * WIDE, i * (2 * WIDE))
        return carry

    def rest(i, carry):
        several(WIDE, i * WIDE)
        return carry

    steps = sizes[0, part]
    lax.fori_loop(0, steps // 2, full, 0)
    lax.fori_loop(steps // 2 * 2, steps, rest, 0)


def fetch(pieces, places, sources, sems):
    copies = []
    for n, (piece, place) in enumerate(zip(pieces, places)):
        there = sources.at[pl.ds(place, piece.shape[0])]
        copies.append(pltpu.make_async_copy(piece, there, sems.at[n]))
    for copy in copies:
        copy.start()
    sources[SOURCES] = jnp.zeros((TILE, TILE), jnp.bfloat16)
    return copies


def early_kernel(lists, groups, sizes, blocks, incident, *rest):
    pieces, (total, sources, sems) = rest[:-3], rest[-3:]
    copies = fetch(pieces, EARLY_AT, sources, sems)
    total[...] = incident[...].astype(jnp.float32)
    for copy in copies:
        copy.wait()
    add_pairs(0, lists, groups, sizes, blocks, sources, total)


def finish(tmatrix, total, t):
    field = total[t].astype(jnp.bfloat16)
    return jnp.dot(tmatrix[t], field, preferred_element_type=jnp.float32).astype(jnp.bfloat16)


def late_kernel(lists, groups, sizes, blocks, before, tmatrix, *rest):
    pieces, (coeff, sources, total, sems) = rest[:-4], rest[-4:]
    copies = fetch(pieces, LATE_AT, sources, sems)
    total[...] = before[...]
    for copy in copies:
        copy.wait()
    add_pairs(1, lists, groups, sizes, blocks, sources, total)
    for t in range(OWN):
        coeff[t] = finish(tmatrix, total, t)


FAR_ROWS = 256
HALF = TILE // 2


def far_kernel(mine, other, coeff, arrived, far):
    def chunk(i, carry):
        rows = pl.ds(pl.multiple_of(i * FAR_ROWS, FAR_ROWS), FAR_ROWS)
        made = dot(mine[rows, :], coeff[...]) + dot(other[rows, :], arrived[...])
        far[rows, :] = made.astype(far.dtype)
        return carry

    lax.fori_loop(0, far.shape[0] // FAR_ROWS, chunk, 0)


def far_field(mine, other, coeff, arrived):
    return pl.pallas_call(
        far_kernel,
        out_shape=jax.ShapeDtypeStruct((mine.shape[0], TILE), jnp.bfloat16),
        in_specs=[VMEM] * 4,
        out_specs=VMEM,
        compiler_params=LIMIT,
        name="far",
    )(mine, other, coeff.reshape(-1, TILE), arrived.reshape(-1, TILE))


def order_kernel(which, owner_far, factor_far, harmonics, ordered, right, owner, factor, sems):
    first = pltpu.make_async_copy(factor_far, factor, sems.at[0])
    first.start()
    copy = pltpu.make_async_copy(harmonics, right.at[:, pl.ds(0, TILE)], sems.at[1])
    copy.start()
    last = pltpu.make_async_copy(owner_far, owner, sems.at[2])
    last.start()
    first.wait()
    for i in range(right.shape[0] // FAR_ROWS):
        rows = pl.ds(i * FAR_ROWS, FAR_ROWS)
        phase = factor[:, rows]
        high = phase.astype(jnp.bfloat16).astype(jnp.float32)
        middle = (phase - high).astype(jnp.bfloat16).astype(jnp.float32)
        parts = [high, middle, phase - high - middle, jnp.zeros_like(phase)]
        parts = jnp.concatenate(parts, axis=0).T
        parts = jnp.concatenate([parts, jnp.zeros((FAR_ROWS, TILE - 4 * OWN), jnp.float32)], axis=1)
        right[rows, TILE:] = parts.astype(jnp.bfloat16)
    copy.wait()
    last.wait()

    def chunk(i, carry):
        rows = pl.ds(pl.multiple_of(i * FAR_ROWS, FAR_ROWS), FAR_ROWS)
        wanted = []
        for n in range(FAR_ROWS // HALF):
            line = owner[pl.ds(i * (FAR_ROWS // HALF) + n, 1), :]
            both = jnp.broadcast_to(line, (TILE, TILE)).T.reshape(HALF // 8, 2, 8, TILE)
            mine = jnp.where(which[0] == 0, both[:, 0], both[:, 1])
            wanted.append(mine.reshape(HALF, TILE))
        wanted = jnp.concatenate(wanted, axis=0)
        place = counted(wanted.shape, 1)
        pick = [ones_where(wanted == place + k) for k in range(0, right.shape[0], TILE)]
        found = dot(jnp.concatenate(pick, axis=1), right[...])
        mode, parts = found[:, :TILE], found[:, TILE:]
        for s in range(OWN):
            phase = parts[:, s : s + 1] + parts[:, OWN + s : OWN + s + 1]
            phase = phase + parts[:, 2 * OWN + s : 2 * OWN + s + 1]
            made = jnp.broadcast_to(phase, mode.shape) * mode
            ordered[rows, s * TILE : (s + 1) * TILE] = made.astype(jnp.bfloat16)
        return carry

    lax.fori_loop(0, ordered.shape[0] // FAR_ROWS, chunk, 0)


def in_order(which, owner, factor, harmonics):
    return pl.pallas_call(
        order_kernel,
        out_shape=jax.ShapeDtypeStruct((owner.shape[0] // 2, OWN * TILE), jnp.bfloat16),
        in_specs=[SMEM] + [HBM] * 3,
        out_specs=VMEM,
        scratch_shapes=[
            pltpu.VMEM((harmonics.shape[0], 2 * TILE), jnp.bfloat16),
            pltpu.VMEM((owner.shape[0] // TILE, TILE), owner.dtype),
            pltpu.VMEM(factor.shape, factor.dtype),
            pltpu.SemaphoreType.DMA((3,)),
        ],
        compiler_params=LIMIT,
        cost_estimate=pl.CostEstimate(
            flops=2_000_000_000, bytes_accessed=4_000_000, transcendentals=0
        ),
        name="order",
    )(which.reshape(1), stay(owner.reshape(-1, TILE)), stay(factor), stay(harmonics))


SCRATCH = pltpu.VMEM((SOURCES + 1, TILE, TILE), jnp.bfloat16)
TOTAL = (OWN, TILE, TILE)


def early_pairs(made, blocks, incident, pieces):
    return pl.pallas_call(
        early_kernel,
        out_shape=jax.ShapeDtypeStruct(TOTAL, jnp.float32),
        in_specs=[SMEM] * 3 + [VMEM] * 2 + [ANY] * len(pieces),
        out_specs=VMEM,
        scratch_shapes=[SCRATCH, pltpu.SemaphoreType.DMA((len(pieces),))],
        cost_estimate=pl.CostEstimate(
            flops=2_000_000_000, bytes_accessed=8_000_000, transcendentals=0
        ),
        compiler_params=LIMIT,
        name="early",
    )(*made, blocks, incident, *pieces)


def late_pairs(made, blocks, before, tmatrix, pieces):
    return pl.pallas_call(
        late_kernel,
        out_shape=jax.ShapeDtypeStruct(TOTAL, jnp.bfloat16),
        in_specs=[SMEM] * 3 + [VMEM] * 3 + [ANY] * len(pieces),
        out_specs=VMEM,
        scratch_shapes=[
            SCRATCH,
            pltpu.VMEM(TOTAL, jnp.float32),
            pltpu.SemaphoreType.DMA((len(pieces),)),
        ],
        compiler_params=LIMIT,
        name="late",
    )(*made, blocks, before, tmatrix, *pieces)


def apply_tmatrix(tmatrix, field):
    product = jnp.einsum("skl,slq->skq", tmatrix, field, preferred_element_type=jnp.float32)
    return product.astype(jnp.bfloat16)


def body(
    incident,
    tmatrix,
    blocks,
    need,
    pair_src,
    pair_tgt,
    pair_blk,
    pair_count,
    factor,
    harmonics,
    owner,
):
    n_grp, n_dev = lax.axis_size("grp"), lax.axis_size("dev")
    coeff = apply_tmatrix(tmatrix, incident)
    made = plan(need[0].T, pair_src, pair_tgt, pair_blk, pair_count)

    rows = owner.shape[0] // (n_grp * n_dev)
    core = lax.axis_index("dev") & 1
    for_other = in_order(1 - core, owner, factor, harmonics)
    near, other, far = spread(coeff, (for_other,), (made,))
    near, other, for_other = lax.optimization_barrier((near, other, for_other))
    weighted_other = send(for_other, SWAP)
    before = early_pairs(made, blocks, incident, near + other)
    before = together(before, weighted_other)
    coeff = late_pairs(made, blocks, before, tmatrix, swapped(far, before))

    mine = in_order(core, owner, factor, harmonics)
    near, other, far = spread(coeff, (mine,), ())
    before = early_pairs(made, blocks, incident, near + other)
    coeff = late_pairs(made, blocks, before, tmatrix, swapped(far, before))

    amplitude = far_field(mine, weighted_other, coeff, send(coeff, SWAP))
    amplitude = amplitude.reshape(n_grp * n_dev // 2, rows, TILE)
    groups = [[g * n_dev + d for g in range(n_grp) for d in same] for same in SAME_CORE]
    amplitude = lax.all_to_all(amplitude, ("grp", "dev"), 0, 0, axis_index_groups=groups)
    return amplitude.astype(jnp.float32).sum(axis=0)


def solution(mesh):
    both = ("grp", "dev")
    return jax.shard_map(
        body,
        mesh=mesh,
        in_specs=(
            P(both, None, None),
            P(both, None, None),
            P(both, None, None),
            P(both, None, None),
            P(both, None),
            P(both, None),
            P(both, None),
            P(both),
            P(both, None),
            P(),
            P(),
        ),
        out_specs=P(both, None),
        check_vma=False,
    )
```
